256 devices in a mesh: view: 16 (over x, z_hi), tile: 16 (over y, z_lo, core).
Axes of the slice: x: 4, y: 4, z: 8 (z_hi: 4, z_lo: 2; z = z_hi * 2 + z_lo), core: 2. Of those that a mesh axis runs over, the one named last changes fastest.
Arguments:
- ref_feat: bfloat16 [32, 32768], P(None, 'tile'), may hold values from -6 to 6
- src_feat: bfloat16 [16, 16, 32, 6144], P('view', 'tile'), may hold values from -6 to 6
- taps: int32 [16, 128, 16], P('view', None, 'tile'), may hold values from 0 to 3838, as said below
- weights: bfloat16 [16, 128, 4, 32768], P('view', None, None, 'tile'), may hold values from 0 to 1, as said below
- conv_weight: float32 [3, 3, 3, 8], replicated, may hold values from -0.4375 to 0.4375
Outputs:
- log_prob: float32 [128, 32768], P('view', 'tile')
- depth_map: float32 [32768], P('tile')
The draws below stay inside these ranges and needn't reach their ends.
Inputs may be any that keep to these rules, and one draw needn't show every extreme that they name: Every offset keeps all four taps of every pixel of the band inside the band's window. For each view, plane and pixel the four weights are (1 - a)(1 - b), a(1 - b), (1 - a) b, a b for some a, b in 0 to 1, rounded to bfloat16.
All inputs are finite; a program needn't handle non-finite values.
Results may differ from the reference program's by a relative error of at most 0.0003.
Values sent between devices are 32-bit elements; how exact they have to be, the bound alone decides.
No kernel may reach another device: no remote copies, remote signals or barrier semaphores. Data moves between devices by JAX's collectives and lax.ppermute only.
A program may use at most 128 MiB of HBM per device.

```python
import jax
import jax.numpy as jnp
from jax import lax

C = 32
G = 8
D = 128
ROWS = 8
COLS = 256
SRC_ROWS = 24
Q = 6144
VIEWS = 16
TILES = 16
PIX = 32768


def draw_taps(key, part):
    keys = jax.random.split(key, 3)
    top_offset = (SRC_ROWS - ROWS - 1) * COLS - 2
    row_shift = jax.random.randint(keys[0], (VIEWS, D, TILES), 0, SRC_ROWS - ROWS - 1)
    disparity = jax.random.randint(keys[1], (VIEWS, 1, 1), 0, COLS // 2)
    col_shift = jnp.arange(D, dtype=jnp.int32)[None, :, None] * disparity // D + jax.random.randint(keys[2], (VIEWS, D, TILES), 0, COLS // 2)
    offset = jnp.clip(row_shift * COLS + col_shift, 0, top_offset).astype(jnp.int32)
    offset = offset.at[0, 0, 0].set(top_offset)
    offset = offset.at[0, 1, 0].set(0)
    return offset


def draw_weights(key, part):
    keys = jax.random.split(key, 2)
    frac_col = jax.random.uniform(keys[0], (VIEWS, D, 1, PIX), jnp.float32)
    frac_row = jax.random.uniform(keys[1], (VIEWS, D, 1, PIX), jnp.float32)
    stacked = jnp.concatenate([(1.0 - frac_col) * (1.0 - frac_row), frac_col * (1.0 - frac_row), (1.0 - frac_col) * frac_row, frac_col * frac_row], axis=2)
    return stacked.astype(jnp.bfloat16)


def level_of(stream_key, dims, cuts, smallest, largest):
    loudness, own = 1.0, jax.random.fold_in(stream_key, 6)
    for axis_at, shards_of in cuts:
        heights = jnp.exp(jax.random.uniform(jax.random.fold_in(own, axis_at), (shards_of,), jnp.float32, smallest / len(cuts), largest / len(cuts)))
        loudness = loudness * jnp.repeat(heights, dims[axis_at] // shards_of).reshape([-1 if axis == axis_at else 1 for axis in range(len(dims))])
    return loudness


def noise(rng, extent, width, limit, pieces=(), held_as=jnp.bfloat16):
    array = width * jax.random.normal(rng, extent, jnp.float32)
    if pieces:
        array = array * level_of(rng, extent, pieces, -0.22, 0.18)
    return jnp.clip(array, -limit, limit).astype(held_as)


def setup_inputs(seed: int = 0) -> dict:
    splits = jax.random.split(jax.random.key(seed), 6)
    return {
        "ref_feat": noise(splits[0], (C, PIX), 1.0, 6.0, ((1, 16),)),
        "src_feat": noise(splits[1], (VIEWS, TILES, C, Q), 1.0, 6.0, ((0, 16), (1, 16))),
        "taps": draw_taps(jax.random.fold_in(splits[5], 71), 0),
        "weights": draw_weights(jax.random.fold_in(splits[5], 71), 0),
        "conv_weight": noise(splits[4], (3, 3, 3, G), (27 * G) ** -0.5, 0.4375, (), jnp.float32),
    }


def correlate_plane(window, ref_values, offset, plane_weights, group_count, col_count):
    pixel_count = ref_values.shape[1]
    chan_count = ref_values.shape[0]
    warped = jnp.zeros((chan_count, pixel_count), jnp.float32)
    shifts = (0, 1, col_count, col_count + 1)
    for tap_index in range(4):
        start = (offset + shifts[tap_index]).astype(jnp.int32)
        cut = lax.dynamic_slice_in_dim(window, start, pixel_count, 1).astype(jnp.float32)
        warped = warped + plane_weights[tap_index].astype(jnp.float32)[None, :] * cut
    products = (ref_values * warped).reshape(group_count, chan_count // group_count, pixel_count)
    return jnp.sum(products, axis=1) / (chan_count // group_count)


def stencil(extended, kernel, depth_count, row_count, col_count):
    result = jnp.zeros((depth_count, row_count, col_count), jnp.float32)
    for shift_d in range(3):
        for shift_r in range(3):
            for shift_c in range(3):
                window_cut = extended[shift_d:shift_d + depth_count, :, shift_r:shift_r + row_count, shift_c:shift_c + col_count]
                result = result + jnp.sum(window_cut * kernel[shift_d, shift_r, shift_c][None, :, None, None], axis=1)
    return result


def reference(ref_feat, src_feat, taps, weights, conv_weight):
    band_pixels = ROWS * COLS
    ref_bands = jnp.transpose(ref_feat.astype(jnp.float32).reshape(C, TILES, band_pixels), (1, 0, 2))

    def view_step(cost_volume, inputs_view):
        source_view, taps_view, weights_view = inputs_view
        weight_bands = weights_view.reshape(D, 4, TILES, band_pixels)

        def plane_step(plane_inputs):
            plane_offsets, plane_weights = plane_inputs
            per_band = jax.vmap(lambda window, ref_band, offset, band_weights: correlate_plane(window, ref_band, offset, band_weights, G, COLS), in_axes=(0, 0, 0, 1))(source_view, ref_bands, plane_offsets, plane_weights)
            return jnp.transpose(per_band, (1, 0, 2)).reshape(G, PIX)

        corr_view = lax.map(plane_step, (taps_view, weight_bands))
        return cost_volume + corr_view, None

    cost_volume, _ = lax.scan(view_step, jnp.zeros((D, G, PIX), jnp.float32), (src_feat, taps, weights))
    row_all = PIX // COLS
    extended = jnp.pad(cost_volume.reshape(D, G, row_all, COLS), ((1, 1), (0, 0), (1, 1), (1, 1)))
    filtered = stencil(extended, conv_weight, D, row_all, COLS)
    logit_value = 4.0 * jnp.tanh(0.5 * filtered)
    exp_values = jnp.exp(logit_value)
    plane_value = jnp.arange(D, dtype=jnp.float32) / (D - 1)
    exp_total = jnp.sum(exp_values, axis=0)
    log_prob = (logit_value - jnp.log(exp_total)[None]).reshape(D, PIX)
    depth_map = (jnp.sum(exp_values * plane_value[:, None, None], axis=0) / exp_total).reshape(PIX)
    return log_prob, depth_map
```

```python
import functools

import jax
import jax.numpy as jnp
from jax import lax
from jax.experimental import pallas as pl
from jax.experimental.pallas import tpu as pltpu
from jax.sharding import PartitionSpec as P


L = 128
G = 8
CH = 4
TAIL = 8

def kernel(planes, rows, halves, taps_ref, ref_ref, src_ref, w_ref, filt_ref, out_ref,
           win, base, tmp, wf, cost, lhs, acc):
    step = pl.program_id(0)
    strips = rows * halves
    lane = lax.broadcasted_iota(jnp.int32, (G, L), 1)
    span = planes + 2 * TAIL

    @pl.when(step == 0)
    def _():
        def lay(ref, dst, count, scale):
            def one(m, _):
                at = pl.multiple_of(m * L, L)
                tmp[...] = ref[:, pl.ds(at, L)].astype(jnp.float32) * scale
                for i in range(CH):
                    dst[m, i] = tmp[pl.ds(i, G, stride=CH), :]
                return 0
            lax.fori_loop(0, count, one, 0)
        lay(src_ref, win, win.shape[0], 1.0)
        lay(ref_ref, base, strips, 1.0 / CH)
        acc[...] = jnp.zeros_like(acc)
        width = planes * G
        dist = (lax.broadcasted_iota(jnp.int32, (span, width), 1) // G
                - lax.broadcasted_iota(jnp.int32, (span, width), 0) + TAIL)
        for b in range(3):
            for e in range(3):
                block = jnp.zeros((span, width), jnp.float32)
                for a in range(3):
                    row = a * 9 + b * 3 + e
                    block = jnp.where(dist == a - 1, filt_ref[row:row + 1, :], block)
                high = block.astype(jnp.bfloat16)
                low = (block - high.astype(jnp.float32)).astype(jnp.bfloat16)
                at = (b * 3 + e) * span
                lhs[at:at + span, 0:width] = high
                lhs[at:at + span, width:2 * width] = high
                lhs[at:at + span, 2 * width:3 * width] = low

    def plane(d, _):
        off = taps_ref[step * planes + d]
        m0 = off // L
        sl = off - m0 * L
        keep0 = lane >= sl
        keep1 = lane >= sl + 1
        turn0 = lax.rem(L - sl, L)
        turn1 = lax.rem(L + L - 1 - sl, L)
        wf[0:4, :] = w_ref[d].astype(jnp.float32)
        at = pl.multiple_of(d * G, G)
        us, vs = [], []
        for r in range(strips + halves):
            u, v = [], []
            for i in range(CH):
                here, after = win[m0 + r, i], win[m0 + r + 1, i]
                u.append(pltpu.roll(jnp.where(keep0, here, after), turn0, axis=1))
                v.append(pltpu.roll(jnp.where(keep1, here, after), turn1, axis=1))
            us.append(u)
            vs.append(v)
            j = r - halves
            if j < 0:
                continue
            total = None
            for k, taps in enumerate((us[j], vs[j], us[r], vs[r])):
                part = base[j, 0] * taps[0]
                for i in range(1, CH):
                    part = part + base[j, i] * taps[i]
                scale = jnp.broadcast_to(wf[k:k + 1, j * L:(j + 1) * L], (G, L))
                part = part * scale
                total = part if total is None else total + part
            cost[pl.ds(at, G), j * L:(j + 1) * L] = total
        return 0

    lax.fori_loop(0, planes, plane, 0)

    cols = halves * L
    edge = lax.broadcasted_iota(jnp.int32, (span, cols), 1)
    put = pl.multiple_of(step * planes, planes)
    for r in range(rows):
        block = cost[:, r * cols:(r + 1) * cols]
        high = block.astype(jnp.bfloat16)
        low = (block - high.astype(jnp.float32)).astype(jnp.bfloat16)
        res = jnp.dot(lhs[...], jnp.concatenate([high, low, high], axis=0), preferred_element_type=jnp.float32)
        for b in range(3):
            part = [res[(b * 3 + e) * span:(b * 3 + e + 1) * span] for e in range(3)]
            s = part[1]
            s = s + jnp.where(edge == 0, 0.0, pltpu.roll(part[0], 1, axis=1))
            s = s + jnp.where(edge == cols - 1, 0.0, pltpu.roll(part[2], cols - 1, axis=1))
            line = r - b + 2
            acc[line, pl.ds(put, span), :] += s

    @pl.when(step == pl.num_programs(0) - 1)
    def _():
        count = out_ref.shape[0]
        for line in range(rows + 2):
            out_ref[:, line * cols:(line + 1) * cols] = acc[line, TAIL:TAIL + count, :]


def partial_filter(ref_feat, window, offsets, weights, conv_weight, planes=32, interpret=False):
    depth, _, pixels = weights.shape
    chans, q = window.shape
    halves = 2
    rows = pixels // (L * halves)
    cols = halves * L
    filt = jnp.tile(conv_weight.reshape(27, G), (1, planes))
    span = planes + 2 * TAIL
    grid_spec = pltpu.PrefetchScalarGridSpec(
        num_scalar_prefetch=1,
        grid=(depth // planes,),
        in_specs=[
            pl.BlockSpec((chans, pixels), lambda c, t: (0, 0)),
            pl.BlockSpec((chans, q), lambda c, t: (0, 0)),
            pl.BlockSpec((planes, 4, pixels), lambda c, t: (c, 0, 0)),
            pl.BlockSpec((27, planes * G), lambda c, t: (0, 0)),
        ],
        out_specs=pl.BlockSpec((depth, (rows + 2) * cols), lambda c, t: (0, 0)),
        scratch_shapes=[
            pltpu.VMEM((q // L, CH, G, L), jnp.float32),
            pltpu.VMEM((pixels // L, CH, G, L), jnp.float32),
            pltpu.VMEM((chans, L), jnp.float32),
            pltpu.VMEM((8, pixels), jnp.float32),
            pltpu.VMEM((planes * G, pixels), jnp.float32),
            pltpu.VMEM((9 * span, 3 * planes * G), jnp.bfloat16),
            pltpu.VMEM((rows + 2, depth + 2 * TAIL, cols), jnp.float32),
        ],
    )
    return pl.pallas_call(
        functools.partial(kernel, planes, rows, halves),
        out_shape=jax.ShapeDtypeStruct((depth, (rows + 2) * cols), jnp.float32),
        grid_spec=grid_spec,
        interpret=interpret,
        name="partial_filter",
    )(offsets, ref_feat, window, weights, filt)


SIDE = 4


def view_shift(value, by_outer, by_inner):
    pairs = [
        (o * SIDE + i, (o + by_outer) % SIDE * SIDE + (i + by_inner) % SIDE)
        for o in range(SIDE)
        for i in range(SIDE)
    ]
    return lax.ppermute(value, "view", pairs)


def scatter_stage(value, mine, outer):
    parts = value.reshape(SIDE, value.shape[0] // SIDE, *value.shape[1:])
    total = lax.dynamic_index_in_dim(parts, mine, 0, False)
    for by in (2, 1, 3):
        away = lax.dynamic_index_in_dim(parts, (mine + by) % SIDE, 0, False)
        total = total + view_shift(away, *((by, 0) if outer else (0, by)))
    return total


def sum_stage(value, outer):
    total = value
    for by in (2, 1, 3):
        total = total + view_shift(value, *((by, 0) if outer else (0, by)))
    return total


def on_device(ref_feat, src_feat, taps, weights, conv_weight):
    depth = taps.shape[1]
    pixels = ref_feat.shape[1]
    cols = 2 * L
    partial = partial_filter(ref_feat, src_feat[0, 0], taps[0, :, 0], weights[0], conv_weight)
    view = lax.axis_index("view")
    slab = scatter_stage(partial, view // SIDE, True)
    slab = scatter_stage(slab, view % SIDE, False)
    tiles = lax.axis_size("tile")
    up = lax.ppermute(slab[:, :cols], "tile", [(t + 1, t) for t in range(tiles - 1)])
    down = lax.ppermute(slab[:, cols + pixels:], "tile", [(t, t + 1) for t in range(tiles - 1)])
    filtered = slab[:, cols:cols + pixels]
    filtered = filtered + jnp.pad(down, ((0, 0), (0, pixels - cols))) + jnp.pad(up, ((0, 0), (pixels - cols, 0)))
    logit = 4.0 * jnp.tanh(0.5 * filtered)
    ex = jnp.exp(logit)
    slab_size = filtered.shape[0]
    plane = (view * slab_size + lax.iota(jnp.int32, slab_size)).astype(jnp.float32) / (depth - 1)
    sums = jnp.stack([jnp.sum(ex, axis=0), jnp.sum(ex * plane[:, None], axis=0)])
    sums = sum_stage(sum_stage(sums, True), False)
    return logit - jnp.log(sums[0])[None], sums[1] / sums[0]


def solution(mesh):
    placed = (
        P(None, "tile"),
        P("view", "tile", None, None),
        P("view", None, "tile"),
        P("view", None, None, "tile"),
        P(),
    )
    return jax.shard_map(
        on_device,
        mesh=mesh,
        in_specs=placed,
        out_specs=(P("view", "tile"), P("tile")),
        check_vma=False,
    )
```

```python
import functools

import jax
import jax.numpy as jnp
from jax import lax
from jax.experimental import pallas as pl
from jax.experimental.pallas import tpu as pltpu
from jax.sharding import PartitionSpec as P


L = 128
G = 8
CH = 4
HALVES = 2
COLS = HALVES * L
GROUP = 8
PACK = 16
SIDE = 4


def block_kernel(turns, scal_ref, ref_hbm, src_hbm, w_hbm, filt_ref, *refs):
    outs, refs = refs[:len(turns)], refs[len(turns):]
    (ref_ref, src_ref, win, base, tmp, wbuf, wf, high, low, lhs, slide, out_ref, sem) = refs
    depth = w_hbm.shape[0]
    count = out_ref.shape[0]
    step = pl.program_id(0)
    held = wbuf.shape[1]
    strips = base.shape[0]
    rows = strips // HALVES

    def span_of(turn):
        block = lax.rem(scal_ref[depth] + turn, SIDE)
        first = block * count - 1
        return block, first, jnp.clip(first, 0, depth - held)

    def fetch(n):
        return pltpu.make_async_copy(w_hbm.at[pl.ds(span_of(turns[n])[2], held)], wbuf.at[n], sem.at[n + 2])

    turn = turns[0]
    for n in range(1, len(turns)):
        turn = jnp.where(step == n, turns[n], turn)
    block, first, start = span_of(turn)

    width = (GROUP + 2) * G

    @pl.when(step == 0)
    def _():
        get_src = pltpu.make_async_copy(src_hbm, src_ref, sem.at[0])
        get_ref = pltpu.make_async_copy(ref_hbm, ref_ref, sem.at[1])
        get_src.start()
        get_ref.start()
        for n in range(len(turns)):
            fetch(n).start()
        batch = tmp.shape[0]

        def regroup(ref, m, u, scale):
            at = pl.multiple_of(m * L, L)
            tmp[u] = ref[:, pl.ds(at, L)].astype(jnp.float32) * scale
            return [tmp[u, pl.ds(i, G, stride=CH), :] for i in range(CH)]

        slide[...] = jnp.zeros_like(slide)
        span = L + PACK
        gap = lax.broadcasted_iota(jnp.int32, (span, L), 0) - lax.broadcasted_iota(jnp.int32, (span, L), 1)

        def lay_slide(n, _):
            slide[n, L:L + span, :] = (gap == n).astype(jnp.float32).astype(jnp.bfloat16)
            return 0

        lax.fori_loop(0, PACK, lay_slide, 0)

        spread = (lax.rem(lax.broadcasted_iota(jnp.int32, (G, width), 1), G)
                  == lax.broadcasted_iota(jnp.int32, (G, width), 0)).astype(jnp.bfloat16)
        dist = (lax.broadcasted_iota(jnp.int32, (GROUP, width), 1) // G
                - lax.broadcasted_iota(jnp.int32, (GROUP, width), 0))
        for b in range(3):
            for e in range(3):
                main = jnp.zeros((GROUP, width), jnp.float32)
                rest = main
                for a in range(3):
                    taps = jnp.broadcast_to(filt_ref[a, b, e:e + 1, :], (G, G))
                    top = taps.astype(jnp.bfloat16)
                    left = (taps - top.astype(jnp.float32)).astype(jnp.bfloat16)
                    wide = jnp.dot(top, spread, preferred_element_type=jnp.float32)
                    fine = jnp.dot(left, spread, preferred_element_type=jnp.float32)
                    main = jnp.where(dist == a, wide, main)
                    rest = jnp.where(dist == a, fine, rest)
                at = (b * 3 + e) * GROUP
                lhs[at:at + GROUP, :] = jnp.concatenate([main, main, rest], axis=1)

        def lay_base(n, _):
            for u in range(batch):
                m = n * batch + u
                for i, part in enumerate(regroup(ref_ref, m, u, 1.0 / CH)):
                    base[m, i] = part
            return 0

        get_ref.wait()
        lax.fori_loop(0, strips // batch, lay_base, 0)

        def lay_window(n, _):
            for u in range(batch):
                m = n * batch + u
                strip = jnp.concatenate(regroup(src_ref, m, u, 1.0), axis=0).astype(jnp.bfloat16)
                win[m + 1, :, 0:L] = strip
                win[m, :, L:2 * L] = strip
            return 0

        get_src.wait()
        lax.fori_loop(0, (win.shape[0] - 1) // batch, lay_window, 0)

    for n in range(len(turns)):
        @pl.when(step == n)
        def _():
            fetch(n).wait()


    def aligner_of(by):
        whole = by // PACK
        at = pl.multiple_of(L - whole * PACK, PACK)
        return slide[by - whole * PACK, pl.ds(at, 2 * L), :]

    def plane(i, slot):
        at = jnp.clip(first + i, 0, depth - 1)
        off = scal_ref[at]
        m0 = off // L
        sl = off - m0 * L
        wf[slot, 0:4, :] = w_pick(at - start)
        aligner = jnp.concatenate([aligner_of(sl), aligner_of(sl + 1)], axis=1)
        count_r = strips + HALVES
        source = win[pl.ds(m0 + 1, count_r)].reshape(count_r * CH * G, 2 * L)
        moved = jnp.dot(source, aligner, preferred_element_type=jnp.float32)
        us, vs, sums = [], [], []
        for r in range(count_r):
            us.append([moved[(r * CH + c) * G:(r * CH + c + 1) * G, 0:L] for c in range(CH)])
            vs.append([moved[(r * CH + c) * G:(r * CH + c + 1) * G, L:2 * L] for c in range(CH)])
            j = r - HALVES
            if j < 0:
                continue
            total = None
            for k, taps in enumerate((us[j], vs[j], us[r], vs[r])):
                part = base[j, 0] * taps[0]
                for c in range(1, CH):
                    part = part + base[j, c] * taps[c]
                part = part * jnp.broadcast_to(wf[slot, k:k + 1, j * L:(j + 1) * L], (G, L))
                total = part if total is None else total + part
            sums.append(total)
        return sums

    def w_pick(at):
        return wbuf[step, at].astype(jnp.float32)

    def pair(p, slot):
        one = plane(2 * p, slot)
        two = plane(2 * p + 1, slot + 1)
        at = pl.multiple_of(p * 2 * G, 2 * G)
        for j in range(strips):
            both = jnp.concatenate([one[j], two[j]], axis=0)
            top = both.astype(jnp.bfloat16)
            high[pl.ds(at, 2 * G), j * L:(j + 1) * L] = top
            low[pl.ds(at, 2 * G), j * L:(j + 1) * L] = (both - top.astype(jnp.float32)).astype(jnp.bfloat16)

    edge = lax.broadcasted_iota(jnp.int32, (GROUP, COLS), 1)

    def filter_group(q):
        at = pl.multiple_of(q * GROUP * G, GROUP * G)
        put = pl.multiple_of(q * GROUP, GROUP)
        lines = [None] * (rows + 2)
        matrix = lhs[...].astype(jnp.bfloat16)
        for r in range(rows):
            top = high[pl.ds(at, width), r * COLS:(r + 1) * COLS]
            left = low[pl.ds(at, width), r * COLS:(r + 1) * COLS]
            res = jnp.dot(matrix, jnp.concatenate([top, left, top], axis=0), preferred_element_type=jnp.float32)
            for b in range(3):
                part = [res[(b * 3 + e) * GROUP:(b * 3 + e + 1) * GROUP] for e in range(3)]
                s = part[1]
                s = s + jnp.where(edge == 0, 0.0, pltpu.roll(part[0], 1, axis=1))
                s = s + jnp.where(edge == COLS - 1, 0.0, pltpu.roll(part[2], COLS - 1, axis=1))
                n = r - b + 2
                lines[n] = s if lines[n] is None else lines[n] + s
        for n in range(rows + 2):
            out_ref[pl.ds(put, GROUP), n * COLS:(n + 1) * COLS] = lines[n]

    pair(0, 0)

    @pl.when(block == 0)
    def _():
        high[0:G, :] = jnp.zeros((G, high.shape[1]), jnp.bfloat16)
        low[0:G, :] = jnp.zeros((G, high.shape[1]), jnp.bfloat16)

    def body(q, _):
        filter_group(jnp.maximum(q - 1, 0))
        for u in range(GROUP // 2):
            pair(q * (GROUP // 2) + 1 + u, 2 * u)
        return 0

    groups = count // GROUP
    lax.fori_loop(0, groups, body, 0)

    @pl.when(block == SIDE - 1)
    def _():
        end = (count + 2) * G
        high[end - G:end, :] = jnp.zeros((G, high.shape[1]), jnp.bfloat16)
        low[end - G:end, :] = jnp.zeros((G, high.shape[1]), jnp.bfloat16)

    filter_group(groups - 1)
    for n in range(len(turns)):
        @pl.when(step == n)
        def _():
            outs[n][...] = out_ref[...]


def block_filter(turns, scal, ref_feat, window, weights, conv_weight, count):
    _, _, pixels = weights.shape
    chans, q = window.shape
    rows = pixels // COLS
    vmem = pl.BlockSpec(memory_space=pltpu.VMEM)
    held = count + 2
    grid_spec = pltpu.PrefetchScalarGridSpec(
        num_scalar_prefetch=1,
        grid=(len(turns),),
        in_specs=[
            pl.BlockSpec(memory_space=pl.ANY),
            pl.BlockSpec(memory_space=pl.ANY),
            pl.BlockSpec(memory_space=pl.ANY),
            pl.BlockSpec((3, 3, 3, G), lambda c, t: (0, 0, 0, 0)),
        ],
        out_specs=[pl.BlockSpec((count, (rows + 2) * COLS), lambda c, t: (0, 0))] * len(turns),
        scratch_shapes=[
            pltpu.VMEM((chans, pixels), jnp.bfloat16),
            pltpu.VMEM((chans, q), jnp.bfloat16),
            pltpu.VMEM((q // L + 1, chans, 2 * L), jnp.bfloat16),
            pltpu.VMEM((pixels // L, CH, G, L), jnp.float32),
            pltpu.VMEM((8, chans, L), jnp.float32),
            pltpu.VMEM((len(turns), held, 4, pixels), jnp.bfloat16),
            pltpu.VMEM((GROUP, 8, pixels), jnp.float32),
            pltpu.VMEM((held * G, pixels), jnp.bfloat16),
            pltpu.VMEM((held * G, pixels), jnp.bfloat16),
            pltpu.VMEM((9 * GROUP, 3 * (GROUP + 2) * G), jnp.float32),
            pltpu.VMEM((PACK, 3 * L, L), jnp.bfloat16),
            pltpu.VMEM((count, (rows + 2) * COLS), jnp.float32),
            pltpu.SemaphoreType.DMA((2 + len(turns),)),
        ],
    )
    return pl.pallas_call(
        functools.partial(block_kernel, turns),
        out_shape=[jax.ShapeDtypeStruct((count, (rows + 2) * COLS), jnp.float32)] * len(turns),
        grid_spec=grid_spec,
        cost_estimate=pl.CostEstimate(flops=3_000_000_000 * len(turns), bytes_accessed=2_000_000, transcendentals=0),
    )(scal, ref_feat, window, weights, conv_weight)


def view_shift(value, by_outer, by_inner):
    pairs = [
        (o * SIDE + i, (o + by_outer) % SIDE * SIDE + (i + by_inner) % SIDE)
        for o in range(SIDE)
        for i in range(SIDE)
    ]
    return lax.ppermute(value, "view", pairs)


def scatter_stage(value, mine, outer):
    parts = value.reshape(SIDE, value.shape[0] // SIDE, *value.shape[1:])
    total = lax.dynamic_index_in_dim(parts, mine, 0, False)
    for by in (2, 1, 3):
        away = lax.dynamic_index_in_dim(parts, (mine + by) % SIDE, 0, False)
        total = total + view_shift(away, *((by, 0) if outer else (0, by)))
    return total


def sum_stage(value, outer):
    total = value
    for by in (2, 1, 3):
        total = total + view_shift(value, *((by, 0) if outer else (0, by)))
    return total


def on_device(ref_feat, src_feat, taps, weights, conv_weight):
    depth = taps.shape[1]
    pixels = ref_feat.shape[1]
    cols = 2 * L
    view = lax.axis_index("view")
    count = depth // SIDE
    scal = jnp.concatenate([taps[0, :, 0], (view // SIDE).astype(jnp.int32)[None]])
    got = {}
    for turns in ((2,), (1, 3), (0,)):
        parts = block_filter(turns, scal, ref_feat, src_feat[0, 0], weights[0], conv_weight, count)
        scal, *parts = lax.optimization_barrier((scal, *parts))
        for turn, part in zip(turns, parts):
            got[turn] = view_shift(part, turn, 0) if turn else part
    slab = got[0] + got[2] + got[1] + got[3]
    slab = scatter_stage(slab, view % SIDE, False)
    tiles = lax.axis_size("tile")
    up = lax.ppermute(slab[:, :cols], "tile", [(t + 1, t) for t in range(tiles - 1)])
    down = lax.ppermute(slab[:, cols + pixels:], "tile", [(t, t + 1) for t in range(tiles - 1)])
    filtered = slab[:, cols:cols + pixels]
    filtered = filtered + jnp.pad(down, ((0, 0), (0, pixels - cols))) + jnp.pad(up, ((0, 0), (pixels - cols, 0)))
    logit = 4.0 * jnp.tanh(0.5 * filtered)
    ex = jnp.exp(logit)
    slab_size = filtered.shape[0]
    plane = (view * slab_size + lax.iota(jnp.int32, slab_size)).astype(jnp.float32) / (depth - 1)
    sums = jnp.stack([jnp.sum(ex, axis=0), jnp.sum(ex * plane[:, None], axis=0)])
    sums = sum_stage(sum_stage(sums, True), False)
    return logit - jnp.log(sums[0])[None], sums[1] / sums[0]


def solution(mesh):
    placed = (
        P(None, "tile"),
        P("view", "tile", None, None),
        P("view", None, "tile"),
        P("view", None, None, "tile"),
        P(),
    )
    return jax.shard_map(
        on_device,
        mesh=mesh,
        in_specs=placed,
        out_specs=(P("view", "tile"), P("tile")),
        check_vma=False,
    )
```

```python
import functools

import jax
import jax.numpy as jnp
from jax import lax
from jax.experimental import pallas as pl
from jax.experimental.pallas import tpu as pltpu
from jax.sharding import PartitionSpec as P


L = 128
G = 8
CH = 4
HALVES = 2
COLS = HALVES * L
GROUP = 8
PACK = 16
SIDE = 4


def outer_index():
    return lax.axis_index("view") // SIDE


def block_kernel(turns, taps_ref, ref_hbm, src_hbm, w_hbm, filt_hbm, *refs):
    outs, refs = refs[:len(turns)], refs[len(turns):]
    (ref_ref, src_ref, filt_ref, win, base, tmp, wbuf, wf, high, low, lhs, slide, out_ref, sem) = refs
    depth = w_hbm.shape[0]
    count = out_ref.shape[0]
    step = pl.program_id(0)
    held = wbuf.shape[1]
    strips = base.shape[0]
    rows = strips // HALVES

    def span_of(turn):
        block = lax.rem(outer_index() + turn, SIDE)
        first = block * count - 1
        return block, first, jnp.clip(first, 0, depth - held)

    def fetch(n):
        return pltpu.make_async_copy(w_hbm.at[pl.ds(span_of(turns[n])[2], held)], wbuf.at[n], sem.at[n + 3])

    turn = turns[0]
    for n in range(1, len(turns)):
        turn = jnp.where(step == n, turns[n], turn)
    block, first, start = span_of(turn)

    width = (GROUP + 2) * G

    @pl.when(step == 0)
    def _():
        get_src = pltpu.make_async_copy(src_hbm, src_ref, sem.at[0])
        get_ref = pltpu.make_async_copy(ref_hbm, ref_ref, sem.at[1])
        get_filt = pltpu.make_async_copy(filt_hbm, filt_ref, sem.at[2])
        get_filt.start()
        get_src.start()
        get_ref.start()
        for n in range(len(turns)):
            fetch(n).start()
        batch = tmp.shape[0]

        def regroup(ref, m, u, scale):
            at = pl.multiple_of(m * L, L)
            tmp[u] = ref[:, pl.ds(at, L)].astype(jnp.float32) * scale
            return [tmp[u, pl.ds(i, G, stride=CH), :] for i in range(CH)]

        slide[...] = jnp.zeros_like(slide)
        span = L + PACK
        gap = lax.broadcasted_iota(jnp.int32, (span, L), 0) - lax.broadcasted_iota(jnp.int32, (span, L), 1)

        def lay_slide(n, _):
            slide[n, L:L + span, :] = (gap == n).astype(jnp.float32).astype(jnp.bfloat16)
            return 0

        lax.fori_loop(0, PACK, lay_slide, 0)

        get_filt.wait()
        spread = (lax.rem(lax.broadcasted_iota(jnp.int32, (G, width), 1), G)
                  == lax.broadcasted_iota(jnp.int32, (G, width), 0)).astype(jnp.bfloat16)
        dist = (lax.broadcasted_iota(jnp.int32, (GROUP, width), 1) // G
                - lax.broadcasted_iota(jnp.int32, (GROUP, width), 0))
        for b in range(3):
            for e in range(3):
                main = jnp.zeros((GROUP, width), jnp.float32)
                rest = main
                for a in range(3):
                    taps = jnp.broadcast_to(filt_ref[a, b, e:e + 1, :], (G, G))
                    top = taps.astype(jnp.bfloat16)
                    left = (taps - top.astype(jnp.float32)).astype(jnp.bfloat16)
                    wide = jnp.dot(top, spread, preferred_element_type=jnp.float32)
                    fine = jnp.dot(left, spread, preferred_element_type=jnp.float32)
                    main = jnp.where(dist == a, wide, main)
                    rest = jnp.where(dist == a, fine, rest)
                at = (b * 3 + e) * GROUP
                lhs[at:at + GROUP, :] = jnp.concatenate([main, main, rest], axis=1)

        def lay_base(n, _):
            for u in range(batch):
                m = n * batch + u
                for i, part in enumerate(regroup(ref_ref, m, u, 1.0 / CH)):
                    base[m, i] = part
            return 0

        get_ref.wait()
        lax.fori_loop(0, strips // batch, lay_base, 0)

        def lay_window(n, _):
            for u in range(batch):
                m = n * batch + u
                strip = jnp.concatenate(regroup(src_ref, m, u, 1.0), axis=0).astype(jnp.bfloat16)
                win[m + 1, :, 0:L] = strip
                win[m, :, L:2 * L] = strip
            return 0

        get_src.wait()
        lax.fori_loop(0, (win.shape[0] - 1) // batch, lay_window, 0)

    for n in range(len(turns)):
        @pl.when(step == n)
        def _():
            fetch(n).wait()


    def aligner_of(by):
        whole = by // PACK
        at = pl.multiple_of(L - whole * PACK, PACK)
        return slide[by - whole * PACK, pl.ds(at, 2 * L), :]

    def plane(i, slot):
        at = jnp.clip(first + i, 0, depth - 1)
        off = taps_ref[at]
        m0 = off // L
        sl = off - m0 * L
        wf[slot, 0:4, :] = w_pick(at - start)
        aligner = jnp.concatenate([aligner_of(sl), aligner_of(sl + 1)], axis=1)
        count_r = strips + HALVES
        source = win[pl.ds(m0 + 1, count_r)].reshape(count_r * CH * G, 2 * L)
        moved = jnp.dot(source, aligner, preferred_element_type=jnp.float32)
        sums = [None] * strips

        def add(j, r, k):
            near = r * CH
            for side in range(2):
                part = None
                for c in range(CH):
                    item = moved[(near + c) * G:(near + c + 1) * G, side * L:(side + 1) * L] * base[j, c]
                    part = item if part is None else part + item
                part = part * jnp.broadcast_to(wf[slot, k + side:k + side + 1, j * L:(j + 1) * L], (G, L))
                sums[j] = part if sums[j] is None else sums[j] + part

        for r in range(count_r):
            if r >= HALVES:
                add(r - HALVES, r, 2)
            if r < strips:
                add(r, r, 0)
        return sums

    def w_pick(at):
        return wbuf[step, at].astype(jnp.float32)

    def pair(p, slot):
        one = plane(2 * p, slot)
        two = plane(2 * p + 1, slot + 1)
        at = pl.multiple_of(p * 2 * G, 2 * G)
        for j in range(strips):
            both = jnp.concatenate([one[j], two[j]], axis=0)
            top = both.astype(jnp.bfloat16)
            high[pl.ds(at, 2 * G), j * L:(j + 1) * L] = top
            low[pl.ds(at, 2 * G), j * L:(j + 1) * L] = (both - top.astype(jnp.float32)).astype(jnp.bfloat16)

    edge = lax.broadcasted_iota(jnp.int32, (GROUP, COLS), 1)

    def finish(lines, n, put):
        total = lines[n, 1]
        total = total + jnp.where(edge == 0, 0.0, pltpu.roll(lines[n, 0], 1, axis=1))
        total = total + jnp.where(edge == COLS - 1, 0.0, pltpu.roll(lines[n, 2], COLS - 1, axis=1))
        out_ref[pl.ds(put, GROUP), n * COLS:(n + 1) * COLS] = total

    def filter_group(q):
        at = pl.multiple_of(q * GROUP * G, GROUP * G)
        put = pl.multiple_of(q * GROUP, GROUP)
        matrix = lhs[...].astype(jnp.bfloat16)
        lines = {}
        for r in range(rows):
            top = high[pl.ds(at, width), r * COLS:(r + 1) * COLS]
            left = low[pl.ds(at, width), r * COLS:(r + 1) * COLS]
            res = jnp.dot(matrix, jnp.concatenate([top, left, top], axis=0), preferred_element_type=jnp.float32)
            for b in range(3):
                for e in range(3):
                    part = res[(b * 3 + e) * GROUP:(b * 3 + e + 1) * GROUP]
                    n = r - b + 2
                    lines[n, e] = lines[n, e] + part if (n, e) in lines else part
            for n in (range(rows, rows + 2) if r == rows - 1 else ()):
                finish(lines, n, put)
            finish(lines, r, put)

    pair(0, 0)

    @pl.when(block == 0)
    def _():
        high[0:G, :] = jnp.zeros((G, high.shape[1]), jnp.bfloat16)
        low[0:G, :] = jnp.zeros((G, high.shape[1]), jnp.bfloat16)

    def body(q, _):
        filter_group(jnp.maximum(q - 1, 0))
        for u in range(GROUP // 2):
            pair(q * (GROUP // 2) + 1 + u, 2 * u)
        return 0

    groups = count // GROUP
    lax.fori_loop(0, groups, body, 0)

    @pl.when(block == SIDE - 1)
    def _():
        end = (count + 2) * G
        high[end - G:end, :] = jnp.zeros((G, high.shape[1]), jnp.bfloat16)
        low[end - G:end, :] = jnp.zeros((G, high.shape[1]), jnp.bfloat16)

    filter_group(groups - 1)
    for n in range(len(turns)):
        @pl.when(step == n)
        def _():
            outs[n][...] = out_ref[...]


def block_filter(turns, offsets, ref_feat, window, weights, conv_weight, count):
    _, _, pixels = weights.shape
    chans, q = window.shape
    rows = pixels // COLS
    vmem = pl.BlockSpec(memory_space=pltpu.VMEM)
    held = count + 2
    grid_spec = pltpu.PrefetchScalarGridSpec(
        num_scalar_prefetch=1,
        grid=(len(turns),),
        in_specs=[
            pl.BlockSpec(memory_space=pl.ANY),
            pl.BlockSpec(memory_space=pl.ANY),
            pl.BlockSpec(memory_space=pl.ANY),
            pl.BlockSpec(memory_space=pl.ANY),
        ],
        out_specs=[pl.BlockSpec((count, (rows + 2) * COLS), lambda c, t: (0, 0))] * len(turns),
        scratch_shapes=[
            pltpu.VMEM((chans, pixels), jnp.bfloat16),
            pltpu.VMEM((chans, q), jnp.bfloat16),
            pltpu.VMEM((3, 3, 3, G), jnp.float32),
            pltpu.VMEM((q // L + 1, chans, 2 * L), jnp.bfloat16),
            pltpu.VMEM((pixels // L, CH, G, L), jnp.float32),
            pltpu.VMEM((8, chans, L), jnp.float32),
            pltpu.VMEM((len(turns), held, 4, pixels), jnp.bfloat16),
            pltpu.VMEM((GROUP, 8, pixels), jnp.float32),
            pltpu.VMEM((held * G, pixels), jnp.bfloat16),
            pltpu.VMEM((held * G, pixels), jnp.bfloat16),
            pltpu.VMEM((9 * GROUP, 3 * (GROUP + 2) * G), jnp.float32),
            pltpu.VMEM((PACK, 3 * L, L), jnp.bfloat16),
            pltpu.VMEM((count, (rows + 2) * COLS), jnp.float32),
            pltpu.SemaphoreType.DMA((3 + len(turns),)),
        ],
    )
    return pl.pallas_call(
        functools.partial(block_kernel, turns),
        out_shape=[jax.ShapeDtypeStruct((count, (rows + 2) * COLS), jnp.float32)] * len(turns),
        grid_spec=grid_spec,
        cost_estimate=pl.CostEstimate(flops=3_000_000_000 * len(turns), bytes_accessed=2_000_000, transcendentals=0),
    )(offsets, ref_feat, window, weights, conv_weight)


def view_shift(value, by_outer, by_inner):
    pairs = [
        (o * SIDE + i, (o + by_outer) % SIDE * SIDE + (i + by_inner) % SIDE)
        for o in range(SIDE)
        for i in range(SIDE)
    ]
    return lax.ppermute(value, "view", pairs)


def scatter_stage(value, mine, outer):
    parts = value.reshape(SIDE, value.shape[0] // SIDE, *value.shape[1:])
    total = lax.dynamic_index_in_dim(parts, mine, 0, False)
    for by in (2, 1, 3):
        away = lax.dynamic_index_in_dim(parts, (mine + by) % SIDE, 0, False)
        total = total + view_shift(away, *((by, 0) if outer else (0, by)))
    return total


def sum_stage(value, outer):
    total = value
    for by in (2, 1, 3):
        total = total + view_shift(value, *((by, 0) if outer else (0, by)))
    return total


def on_device(ref_feat, src_feat, taps, weights, conv_weight):
    depth = taps.shape[1]
    pixels = ref_feat.shape[1]
    cols = 2 * L
    view = lax.axis_index("view")
    count = depth // SIDE
    offsets = taps[0, :, 0]
    got = {}
    for turns in ((2,), (1, 3), (0,)):
        parts = block_filter(turns, offsets, ref_feat, src_feat[0, 0], weights[0], conv_weight, count)
        offsets, *parts = lax.optimization_barrier((offsets, *parts))
        for turn, part in zip(turns, parts):
            got[turn] = view_shift(part, turn, 0) if turn else part
    slab = got[0] + got[2] + got[1] + got[3]
    slab = scatter_stage(slab, view % SIDE, False)
    tiles = lax.axis_size("tile")
    up = lax.ppermute(slab[:, :cols], "tile", [(t + 1, t) for t in range(tiles - 1)])
    down = lax.ppermute(slab[:, cols + pixels:], "tile", [(t, t + 1) for t in range(tiles - 1)])
    filtered = slab[:, cols:cols + pixels]
    filtered = filtered + jnp.pad(down, ((0, 0), (0, pixels - cols))) + jnp.pad(up, ((0, 0), (pixels - cols, 0)))
    logit = 4.0 * jnp.tanh(0.5 * filtered)
    ex = jnp.exp(logit)
    slab_size = filtered.shape[0]
    plane = (view * slab_size + lax.iota(jnp.int32, slab_size)).astype(jnp.float32) / (depth - 1)
    sums = jnp.stack([jnp.sum(ex, axis=0), jnp.sum(ex * plane[:, None], axis=0)])
    sums = sum_stage(sum_stage(sums, True), False)
    return logit - jnp.log(sums[0])[None], sums[1] / sums[0]


def solution(mesh):
    placed = (
        P(None, "tile"),
        P("view", "tile", None, None),
        P("view", None, "tile"),
        P("view", None, None, "tile"),
        P(),
    )
    return jax.shard_map(
        on_device,
        mesh=mesh,
        in_specs=placed,
        out_specs=(P("view", "tile"), P("tile")),
        check_vma=False,
    )
```

```python
import functools

import jax
import jax.numpy as jnp
from jax import lax
from jax.experimental import pallas as pl
from jax.experimental.pallas import tpu as pltpu
from jax.sharding import PartitionSpec as P


L = 128
G = 8
CH = 4
HALVES = 2
COLS = HALVES * L
GROUP = 8
PACK = 16
SIDE = 4


def outer_index():
    return lax.axis_index("view") // SIDE


def block_kernel(turns, taps_ref, ref_hbm, src_hbm, w_hbm, filt_hbm, *refs):
    outs, refs = refs[:len(turns)], refs[len(turns):]
    (ref_ref, src_ref, filt_ref, win, base, tmp, wbuf, wf, high, low, lhs, slide, out_ref, sem) = refs
    depth = w_hbm.shape[0]
    count = out_ref.shape[0]
    step = pl.program_id(0)
    held = wbuf.shape[1]
    strips = base.shape[0]
    rows = strips // HALVES

    def span_of(turn):
        block = lax.rem(outer_index() + turn, SIDE)
        first = block * count - 1
        return block, first, jnp.clip(first, 0, depth - held)

    def fetch(n):
        return pltpu.make_async_copy(w_hbm.at[pl.ds(span_of(turns[n])[2], held)], wbuf.at[n], sem.at[n + 3])

    turn = turns[0]
    for n in range(1, len(turns)):
        turn = jnp.where(step == n, turns[n], turn)
    block, first, start = span_of(turn)

    width = (GROUP + 2) * G

    @pl.when(step == 0)
    def _():
        get_src = pltpu.make_async_copy(src_hbm, src_ref, sem.at[0])
        get_ref = pltpu.make_async_copy(ref_hbm, ref_ref, sem.at[1])
        get_filt = pltpu.make_async_copy(filt_hbm, filt_ref, sem.at[2])
        get_filt.start()
        get_src.start()
        get_ref.start()
        for n in range(len(turns)):
            fetch(n).start()
        batch = tmp.shape[0]

        def regroup(ref, m, u, scale):
            at = pl.multiple_of(m * L, L)
            tmp[u] = ref[:, pl.ds(at, L)].astype(jnp.float32) * scale
            return [tmp[u, pl.ds(i, G, stride=CH), :] for i in range(CH)]

        slide[...] = jnp.zeros_like(slide)
        span = L + PACK
        gap = lax.broadcasted_iota(jnp.int32, (span, L), 0) - lax.broadcasted_iota(jnp.int32, (span, L), 1)

        def lay_slide(n, _):
            slide[n, L:L + span, :] = (gap == n).astype(jnp.float32).astype(jnp.bfloat16)
            return 0

        lax.fori_loop(0, PACK, lay_slide, 0)

        get_filt.wait()
        spread = (lax.rem(lax.broadcasted_iota(jnp.int32, (G, width), 1), G)
                  == lax.broadcasted_iota(jnp.int32, (G, width), 0)).astype(jnp.bfloat16)
        dist = (lax.broadcasted_iota(jnp.int32, (GROUP, width), 1) // G
                - lax.broadcasted_iota(jnp.int32, (GROUP, width), 0))
        for b in range(3):
            for e in range(3):
                main = jnp.zeros((GROUP, width), jnp.float32)
                rest = main
                for a in range(3):
                    taps = jnp.broadcast_to(filt_ref[a, b, e:e + 1, :], (G, G))
                    top = taps.astype(jnp.bfloat16)
                    left = (taps - top.astype(jnp.float32)).astype(jnp.bfloat16)
                    wide = jnp.dot(top, spread, preferred_element_type=jnp.float32)
                    fine = jnp.dot(left, spread, preferred_element_type=jnp.float32)
                    main = jnp.where(dist == a, wide, main)
                    rest = jnp.where(dist == a, fine, rest)
                at = (b * 3 + e) * GROUP
                lhs[at:at + GROUP, :] = jnp.concatenate([main, main, rest], axis=1)

        def lay_base(n, _):
            for u in range(batch):
                m = n * batch + u
                for i, part in enumerate(regroup(ref_ref, m, u, 1.0 / CH)):
                    base[m, i] = part
            return 0

        get_ref.wait()
        lax.fori_loop(0, strips // batch, lay_base, 0)

        def lay_window(n, _):
            for u in range(batch):
                m = n * batch + u
                strip = jnp.concatenate(regroup(src_ref, m, u, 1.0), axis=0).astype(jnp.bfloat16)
                win[m + 1, :, 0:L] = strip
                win[m, :, L:2 * L] = strip
            return 0

        get_src.wait()
        lax.fori_loop(0, (win.shape[0] - 1) // batch, lay_window, 0)

    for n in range(len(turns)):
        @pl.when(step == n)
        def _():
            fetch(n).wait()


    def aligner_of(by):
        whole = by // PACK
        at = pl.multiple_of(L - whole * PACK, PACK)
        return slide[by - whole * PACK, pl.ds(at, 2 * L), :]

    def plane(i, slot):
        at = jnp.clip(first + i, 0, depth - 1)
        off = taps_ref[at]
        m0 = off // L
        sl = off - m0 * L
        wf[slot, 0:4, :] = w_pick(at - start)
        aligner = jnp.concatenate([aligner_of(sl), aligner_of(sl + 1)], axis=1)
        count_r = strips + HALVES
        source = win[pl.ds(m0 + 1, count_r)].reshape(count_r * CH * G, 2 * L)
        moved = jnp.dot(source, aligner, preferred_element_type=jnp.float32)
        sums = [None] * strips

        def add(j, r, k):
            near = r * CH
            for side in range(2):
                part = None
                for c in range(CH):
                    item = moved[(near + c) * G:(near + c + 1) * G, side * L:(side + 1) * L] * base[j, c]
                    part = item if part is None else part + item
                part = part * jnp.broadcast_to(wf[slot, k + side:k + side + 1, j * L:(j + 1) * L], (G, L))
                sums[j] = part if sums[j] is None else sums[j] + part

        for r in range(count_r):
            if r >= HALVES:
                add(r - HALVES, r, 2)
            if r < strips:
                add(r, r, 0)
        return sums

    def w_pick(at):
        return wbuf[step, at].astype(jnp.float32)

    def pair(p, slot):
        one = plane(2 * p, slot)
        two = plane(2 * p + 1, slot + 1)
        at = pl.multiple_of(p * 2 * G, 2 * G)
        for j in range(strips):
            both = jnp.concatenate([one[j], two[j]], axis=0)
            top = both.astype(jnp.bfloat16)
            high[pl.ds(at, 2 * G), j * L:(j + 1) * L] = top
            low[pl.ds(at, 2 * G), j * L:(j + 1) * L] = (both - top.astype(jnp.float32)).astype(jnp.bfloat16)

    edge = lax.broadcasted_iota(jnp.int32, (GROUP, COLS), 1)

    def finish(lines, n, put):
        total = lines[n, 1]
        total = total + jnp.where(edge == 0, 0.0, pltpu.roll(lines[n, 0], 1, axis=1))
        total = total + jnp.where(edge == COLS - 1, 0.0, pltpu.roll(lines[n, 2], COLS - 1, axis=1))
        out_ref[pl.ds(put, GROUP), n * COLS:(n + 1) * COLS] = total

    def filter_group(q):
        at = pl.multiple_of(q * GROUP * G, GROUP * G)
        put = pl.multiple_of(q * GROUP, GROUP)
        matrix = lhs[...].astype(jnp.bfloat16)
        lines = {}
        for r in range(rows):
            top = high[pl.ds(at, width), r * COLS:(r + 1) * COLS]
            left = low[pl.ds(at, width), r * COLS:(r + 1) * COLS]
            res = jnp.dot(matrix, jnp.concatenate([top, left, top], axis=0), preferred_element_type=jnp.float32)
            for b in range(3):
                for e in range(3):
                    part = res[(b * 3 + e) * GROUP:(b * 3 + e + 1) * GROUP]
                    n = r - b + 2
                    lines[n, e] = lines[n, e] + part if (n, e) in lines else part
            for n in (range(rows, rows + 2) if r == rows - 1 else ()):
                finish(lines, n, put)
            finish(lines, r, put)

    pair(0, 0)

    @pl.when(block == 0)
    def _():
        high[0:G, :] = jnp.zeros((G, high.shape[1]), jnp.bfloat16)
        low[0:G, :] = jnp.zeros((G, high.shape[1]), jnp.bfloat16)

    def body(q, _):
        filter_group(jnp.maximum(q - 1, 0))
        for u in range(GROUP // 2):
            pair(q * (GROUP // 2) + 1 + u, 2 * u)
        return 0

    groups = count // GROUP
    lax.fori_loop(0, groups, body, 0)

    @pl.when(block == SIDE - 1)
    def _():
        end = (count + 2) * G
        high[end - G:end, :] = jnp.zeros((G, high.shape[1]), jnp.bfloat16)
        low[end - G:end, :] = jnp.zeros((G, high.shape[1]), jnp.bfloat16)

    filter_group(groups - 1)
    for n in range(len(turns)):
        @pl.when(step == n)
        def _():
            outs[n][...] = out_ref[...]


def block_filter(turns, offsets, ref_feat, window, weights, conv_weight, count):
    _, _, pixels = weights.shape
    chans, q = window.shape
    rows = pixels // COLS
    vmem = pl.BlockSpec(memory_space=pltpu.VMEM)
    held = count + 2
    grid_spec = pltpu.PrefetchScalarGridSpec(
        num_scalar_prefetch=1,
        grid=(len(turns),),
        in_specs=[
            pl.BlockSpec(memory_space=pl.ANY),
            pl.BlockSpec(memory_space=pl.ANY),
            pl.BlockSpec(memory_space=pl.ANY),
            pl.BlockSpec(memory_space=pl.ANY),
        ],
        out_specs=[pl.BlockSpec((count, (rows + 2) * COLS), lambda c, t: (0, 0))] * len(turns),
        scratch_shapes=[
            pltpu.VMEM((chans, pixels), jnp.bfloat16),
            pltpu.VMEM((chans, q), jnp.bfloat16),
            pltpu.VMEM((3, 3, 3, G), jnp.float32),
            pltpu.VMEM((q // L + 1, chans, 2 * L), jnp.bfloat16),
            pltpu.VMEM((pixels // L, CH, G, L), jnp.float32),
            pltpu.VMEM((8, chans, L), jnp.float32),
            pltpu.VMEM((len(turns), held, 4, pixels), jnp.bfloat16),
            pltpu.VMEM((GROUP, 8, pixels), jnp.float32),
            pltpu.VMEM((held * G, pixels), jnp.bfloat16),
            pltpu.VMEM((held * G, pixels), jnp.bfloat16),
            pltpu.VMEM((9 * GROUP, 3 * (GROUP + 2) * G), jnp.float32),
            pltpu.VMEM((PACK, 3 * L, L), jnp.bfloat16),
            pltpu.VMEM((count, (rows + 2) * COLS), jnp.float32),
            pltpu.SemaphoreType.DMA((3 + len(turns),)),
        ],
    )
    return pl.pallas_call(
        functools.partial(block_kernel, turns),
        out_shape=[jax.ShapeDtypeStruct((count, (rows + 2) * COLS), jnp.float32)] * len(turns),
        grid_spec=grid_spec,
        cost_estimate=pl.CostEstimate(flops=3_000_000_000 * len(turns), bytes_accessed=2_000_000, transcendentals=0),
    )(offsets, ref_feat, window, weights, conv_weight)


def view_shift(value, by_outer, by_inner):
    pairs = [
        (o * SIDE + i, (o + by_outer) % SIDE * SIDE + (i + by_inner) % SIDE)
        for o in range(SIDE)
        for i in range(SIDE)
    ]
    return lax.ppermute(value, "view", pairs)


def scatter_stage(value, mine):
    parts = value.reshape(SIDE, value.shape[0] // SIDE, *value.shape[1:])
    total = lax.dynamic_index_in_dim(parts, mine, 0, False)
    for by in (2, 1, 3):
        away = lax.dynamic_index_in_dim(parts, (mine + by) % SIDE, 0, False)
        away = view_shift(away, 0, by)
        total = total + away
    return total


def sum_stage(value, outer):
    total = value
    for by in (2, 1, 3):
        away = view_shift(value, *((by, 0) if outer else (0, by)))
        total = total + away
    return total


def on_device(ref_feat, src_feat, taps, weights, conv_weight):
    depth = taps.shape[1]
    pixels = ref_feat.shape[1]
    cols = 2 * L
    view = lax.axis_index("view")
    count = depth // SIDE
    offsets = taps[0, :, 0]
    got = {}
    for turns in ((2,), (1, 3), (0,)):
        parts = block_filter(turns, offsets, ref_feat, src_feat[0, 0], weights[0], conv_weight, count)
        offsets, *parts = lax.optimization_barrier((offsets, *parts))
        for turn, part in zip(turns, parts):
            got[turn] = view_shift(part, turn, 0) if turn else part
    slab = got[0] + got[2] + got[1] + got[3]
    slab = scatter_stage(slab, view % SIDE)
    tiles = lax.axis_size("tile")
    up = lax.ppermute(slab[:, :cols], "tile", [(t + 1, t) for t in range(tiles - 1)])
    down = lax.ppermute(slab[:, cols + pixels:], "tile", [(t, t + 1) for t in range(tiles - 1)])
    filtered = slab[:, cols:cols + pixels]
    filtered = filtered + jnp.pad(down, ((0, 0), (0, pixels - cols))) + jnp.pad(up, ((0, 0), (pixels - cols, 0)))
    logit = 4.0 * jnp.tanh(0.5 * filtered)
    ex = jnp.exp(logit)
    slab_size = filtered.shape[0]
    plane = (view * slab_size + lax.iota(jnp.int32, slab_size)).astype(jnp.float32) / (depth - 1)
    sums = jnp.stack([jnp.sum(ex, axis=0), jnp.sum(ex * plane[:, None], axis=0)])
    sums = sum_stage(sum_stage(sums, True), False)
    return logit - jnp.log(sums[0])[None], sums[1] / sums[0]


def solution(mesh):
    placed = (
        P(None, "tile"),
        P("view", "tile", None, None),
        P("view", None, "tile"),
        P("view", None, None, "tile"),
        P(),
    )
    return jax.shard_map(
        on_device,
        mesh=mesh,
        in_specs=placed,
        out_specs=(P("view", "tile"), P("tile")),
        check_vma=False,
    )
```

```python
import functools

import jax
import jax.numpy as jnp
from jax import lax
from jax.experimental import pallas as pl
from jax.experimental.pallas import tpu as pltpu
from jax.sharding import PartitionSpec as P


L = 128
G = 8
CH = 4
HALVES = 2
COLS = HALVES * L
GROUP = 8
PACK = 16
SIDE = 4


def outer_index():
    return lax.axis_index("view") // SIDE


def block_kernel(turns, taps_ref, ref_hbm, src_hbm, w_hbm, filt_hbm, *refs):
    outs, refs = refs[:len(turns)], refs[len(turns):]
    (ref_ref, src_ref, filt_ref, win, base, tmp, wbuf, wf, high, low, lhs, slide, held_out, sem) = refs
    out_ref = outs[0] if len(turns) == 1 else held_out
    depth = w_hbm.shape[0]
    count = out_ref.shape[0]
    step = pl.program_id(0)
    held = wbuf.shape[1]
    strips = base.shape[0]
    rows = strips // HALVES

    def span_of(turn):
        block = lax.rem(outer_index() + turn, SIDE)
        first = block * count - 1
        return block, first, jnp.clip(first, 0, depth - held)

    def fetch(n):
        return pltpu.make_async_copy(w_hbm.at[pl.ds(span_of(turns[n])[2], held)], wbuf.at[n], sem.at[n + 3])

    turn = turns[0]
    for n in range(1, len(turns)):
        turn = jnp.where(step == n, turns[n], turn)
    block, first, start = span_of(turn)

    width = (GROUP + 2) * G

    @pl.when(step == 0)
    def _():
        get_src = pltpu.make_async_copy(src_hbm, src_ref, sem.at[0])
        get_ref = pltpu.make_async_copy(ref_hbm, ref_ref, sem.at[1])
        get_filt = pltpu.make_async_copy(filt_hbm, filt_ref, sem.at[2])
        get_filt.start()
        get_src.start()
        get_ref.start()
        for n in range(len(turns)):
            fetch(n).start()
        batch = tmp.shape[0]

        def regroup(ref, m, u, scale):
            at = pl.multiple_of(m * L, L)
            tmp[u] = ref[:, pl.ds(at, L)].astype(jnp.float32) * scale
            return [tmp[u, pl.ds(i, G, stride=CH), :] for i in range(CH)]

        slide[...] = jnp.zeros_like(slide)
        span = L + PACK
        gap = lax.broadcasted_iota(jnp.int32, (span, L), 0) - lax.broadcasted_iota(jnp.int32, (span, L), 1)

        def lay_slide(n, _):
            slide[n, L:L + span, :] = (gap == n).astype(jnp.float32).astype(jnp.bfloat16)
            return 0

        lax.fori_loop(0, PACK, lay_slide, 0)

        get_filt.wait()
        spread = (lax.rem(lax.broadcasted_iota(jnp.int32, (G, width), 1), G)
                  == lax.broadcasted_iota(jnp.int32, (G, width), 0)).astype(jnp.bfloat16)
        dist = (lax.broadcasted_iota(jnp.int32, (GROUP, width), 1) // G
                - lax.broadcasted_iota(jnp.int32, (GROUP, width), 0))
        for b in range(3):
            for e in range(3):
                main = jnp.zeros((GROUP, width), jnp.float32)
                rest = main
                for a in range(3):
                    taps = jnp.broadcast_to(filt_ref[a, b, e:e + 1, :], (G, G))
                    top = taps.astype(jnp.bfloat16)
                    left = (taps - top.astype(jnp.float32)).astype(jnp.bfloat16)
                    wide = jnp.dot(top, spread, preferred_element_type=jnp.float32)
                    fine = jnp.dot(left, spread, preferred_element_type=jnp.float32)
                    main = jnp.where(dist == a, wide, main)
                    rest = jnp.where(dist == a, fine, rest)
                at = (b * 3 + e) * GROUP
                lhs[at:at + GROUP, :] = jnp.concatenate([main, main, rest], axis=1)

        def lay_base(n, _):
            for u in range(batch):
                m = n * batch + u
                for i, part in enumerate(regroup(ref_ref, m, u, 1.0 / CH)):
                    base[m, i] = part
            return 0

        get_ref.wait()
        lax.fori_loop(0, strips // batch, lay_base, 0)

        def lay_window(n, _):
            for u in range(batch):
                m = n * batch + u
                strip = jnp.concatenate(regroup(src_ref, m, u, 1.0), axis=0).astype(jnp.bfloat16)
                win[m + 1, :, 0:L] = strip
                win[m, :, L:2 * L] = strip
            return 0

        get_src.wait()
        lax.fori_loop(0, (win.shape[0] - 1) // batch, lay_window, 0)

    for n in range(len(turns)):
        @pl.when(step == n)
        def _():
            fetch(n).wait()


    def aligner_of(by):
        whole = by // PACK
        at = pl.multiple_of(L - whole * PACK, PACK)
        return slide[by - whole * PACK, pl.ds(at, 2 * L), :]

    def plane(i, slot):
        at = jnp.clip(first + i, 0, depth - 1)
        off = taps_ref[at]
        m0 = off // L
        sl = off - m0 * L
        wf[slot, 0:4, :] = w_pick(at - start)
        aligner = jnp.concatenate([aligner_of(sl), aligner_of(sl + 1)], axis=1)
        count_r = strips + HALVES
        source = win[pl.ds(m0 + 1, count_r)].reshape(count_r * CH * G, 2 * L)
        moved = jnp.dot(source, aligner, preferred_element_type=jnp.float32)
        sums = [None] * strips

        def add(j, r, k):
            near = r * CH
            for side in range(2):
                part = None
                for c in range(CH):
                    item = moved[(near + c) * G:(near + c + 1) * G, side * L:(side + 1) * L] * base[j, c]
                    part = item if part is None else part + item
                part = part * jnp.broadcast_to(wf[slot, k + side:k + side + 1, j * L:(j + 1) * L], (G, L))
                sums[j] = part if sums[j] is None else sums[j] + part

        for r in range(count_r):
            if r >= HALVES:
                add(r - HALVES, r, 2)
            if r < strips:
                add(r, r, 0)
        return sums

    def w_pick(at):
        return wbuf[step, at].astype(jnp.float32)

    def pair(p, slot):
        one = plane(2 * p, slot)
        two = plane(2 * p + 1, slot + 1)
        at = pl.multiple_of(p * 2 * G, 2 * G)
        for j in range(strips):
            both = jnp.concatenate([one[j], two[j]], axis=0)
            top = both.astype(jnp.bfloat16)
            high[pl.ds(at, 2 * G), j * L:(j + 1) * L] = top
            low[pl.ds(at, 2 * G), j * L:(j + 1) * L] = (both - top.astype(jnp.float32)).astype(jnp.bfloat16)

    edge = lax.broadcasted_iota(jnp.int32, (GROUP, COLS), 1)

    def finish(lines, n, put):
        total = lines[n, 1]
        total = total + jnp.where(edge == 0, 0.0, pltpu.roll(lines[n, 0], 1, axis=1))
        total = total + jnp.where(edge == COLS - 1, 0.0, pltpu.roll(lines[n, 2], COLS - 1, axis=1))
        out_ref[pl.ds(put, GROUP), n * COLS:(n + 1) * COLS] = total

    def filter_group(q):
        at = pl.multiple_of(q * GROUP * G, GROUP * G)
        put = pl.multiple_of(q * GROUP, GROUP)
        matrix = lhs[...].astype(jnp.bfloat16)
        lines = {}
        for r in range(rows):
            top = high[pl.ds(at, width), r * COLS:(r + 1) * COLS]
            left = low[pl.ds(at, width), r * COLS:(r + 1) * COLS]
            res = jnp.dot(matrix, jnp.concatenate([top, left, top], axis=0), preferred_element_type=jnp.float32)
            for b in range(3):
                for e in range(3):
                    part = res[(b * 3 + e) * GROUP:(b * 3 + e + 1) * GROUP]
                    n = r - b + 2
                    lines[n, e] = lines[n, e] + part if (n, e) in lines else part
            for n in (range(rows, rows + 2) if r == rows - 1 else ()):
                finish(lines, n, put)
            finish(lines, r, put)

    pair(0, 0)

    @pl.when(block == 0)
    def _():
        high[0:G, :] = jnp.zeros((G, high.shape[1]), jnp.bfloat16)
        low[0:G, :] = jnp.zeros((G, high.shape[1]), jnp.bfloat16)

    def body(q, _):
        filter_group(jnp.maximum(q - 1, 0))
        for u in range(GROUP // 2):
            pair(q * (GROUP // 2) + 1 + u, 2 * u)
        return 0

    groups = count // GROUP
    lax.fori_loop(0, groups, body, 0)

    @pl.when(block == SIDE - 1)
    def _():
        end = (count + 2) * G
        high[end - G:end, :] = jnp.zeros((G, high.shape[1]), jnp.bfloat16)
        low[end - G:end, :] = jnp.zeros((G, high.shape[1]), jnp.bfloat16)

    filter_group(groups - 1)
    for n in range(len(turns) if len(turns) > 1 else 0):
        @pl.when(step == n)
        def _():
            outs[n][...] = out_ref[...]


def block_filter(turns, offsets, ref_feat, window, weights, conv_weight, count):
    _, _, pixels = weights.shape
    chans, q = window.shape
    rows = pixels // COLS
    vmem = pl.BlockSpec(memory_space=pltpu.VMEM)
    held = count + 2
    grid_spec = pltpu.PrefetchScalarGridSpec(
        num_scalar_prefetch=1,
        grid=(len(turns),),
        in_specs=[
            pl.BlockSpec(memory_space=pl.ANY),
            pl.BlockSpec(memory_space=pl.ANY),
            pl.BlockSpec(memory_space=pl.ANY),
            pl.BlockSpec(memory_space=pl.ANY),
        ],
        out_specs=[pl.BlockSpec((count, (rows + 2) * COLS), lambda c, t: (0, 0))] * len(turns),
        scratch_shapes=[
            pltpu.VMEM((chans, pixels), jnp.bfloat16),
            pltpu.VMEM((chans, q), jnp.bfloat16),
            pltpu.VMEM((3, 3, 3, G), jnp.float32),
            pltpu.VMEM((q // L + 1, chans, 2 * L), jnp.bfloat16),
            pltpu.VMEM((pixels // L, CH, G, L), jnp.float32),
            pltpu.VMEM((8, chans, L), jnp.float32),
            pltpu.VMEM((len(turns), held, 4, pixels), jnp.bfloat16),
            pltpu.VMEM((GROUP, 8, pixels), jnp.float32),
            pltpu.VMEM((held * G, pixels), jnp.bfloat16),
            pltpu.VMEM((held * G, pixels), jnp.bfloat16),
            pltpu.VMEM((9 * GROUP, 3 * (GROUP + 2) * G), jnp.float32),
            pltpu.VMEM((PACK, 3 * L, L), jnp.bfloat16),
            pltpu.VMEM((count, (rows + 2) * COLS), jnp.float32),
            pltpu.SemaphoreType.DMA((3 + len(turns),)),
        ],
    )
    return pl.pallas_call(
        functools.partial(block_kernel, turns),
        out_shape=[jax.ShapeDtypeStruct((count, (rows + 2) * COLS), jnp.float32)] * len(turns),
        grid_spec=grid_spec,
        cost_estimate=pl.CostEstimate(flops=3_000_000_000 * len(turns), bytes_accessed=2_000_000, transcendentals=0),
    )(offsets, ref_feat, window, weights, conv_weight)


def view_shift(value, by_outer, by_inner):
    pairs = [
        (o * SIDE + i, (o + by_outer) % SIDE * SIDE + (i + by_inner) % SIDE)
        for o in range(SIDE)
        for i in range(SIDE)
    ]
    return lax.ppermute(value, "view", pairs)


def scatter_stage(value, mine):
    parts = value.reshape(SIDE, value.shape[0] // SIDE, *value.shape[1:])
    total = lax.dynamic_index_in_dim(parts, mine, 0, False)
    for by in (2, 1, 3):
        away = lax.dynamic_index_in_dim(parts, (mine + by) % SIDE, 0, False)
        away = view_shift(away, 0, by)
        total = total + away
    return total


def sum_stage(value, outer):
    total = value
    for by in (2, 1, 3):
        away = view_shift(value, *((by, 0) if outer else (0, by)))
        total = total + away
    return total


def on_device(ref_feat, src_feat, taps, weights, conv_weight):
    depth = taps.shape[1]
    pixels = ref_feat.shape[1]
    cols = 2 * L
    view = lax.axis_index("view")
    count = depth // SIDE
    offsets = taps[0, :, 0]
    got = {}
    for turns in ((2,), (1, 3), (0,)):
        parts = block_filter(turns, offsets, ref_feat, src_feat[0, 0], weights[0], conv_weight, count)
        offsets, *parts = lax.optimization_barrier((offsets, *parts))
        for turn, part in zip(turns, parts):
            got[turn] = view_shift(part, turn, 0) if turn else part
    slab = got[0] + got[2] + got[1] + got[3]
    slab = scatter_stage(slab, view % SIDE)
    tiles = lax.axis_size("tile")
    up = lax.ppermute(slab[:, :cols], "tile", [(t + 1, t) for t in range(tiles - 1)])
    down = lax.ppermute(slab[:, cols + pixels:], "tile", [(t, t + 1) for t in range(tiles - 1)])
    filtered = slab[:, cols:cols + pixels]
    filtered = filtered + jnp.pad(down, ((0, 0), (0, pixels - cols))) + jnp.pad(up, ((0, 0), (pixels - cols, 0)))
    logit = 4.0 * jnp.tanh(0.5 * filtered)
    ex = jnp.exp(logit)
    slab_size = filtered.shape[0]
    plane = (view * slab_size + lax.iota(jnp.int32, slab_size)).astype(jnp.float32) / (depth - 1)
    sums = jnp.stack([jnp.sum(ex, axis=0), jnp.sum(ex * plane[:, None], axis=0)])
    sums = sum_stage(sum_stage(sums, True), False)
    return logit - jnp.log(sums[0])[None], sums[1] / sums[0]


def solution(mesh):
    placed = (
        P(None, "tile"),
        P("view", "tile", None, None),
        P("view", None, "tile"),
        P("view", None, None, "tile"),
        P(),
    )
    return jax.shard_map(
        on_device,
        mesh=mesh,
        in_specs=placed,
        out_specs=(P("view", "tile"), P("tile")),
        check_vma=False,
    )
```
